32 devices in a mesh: slab: 8 (over z, x), sub: 4 (over y, core).
Axes of the slice: x: 2, y: 2, z: 4, core: 2. Of those that a mesh axis runs over, the one named last changes fastest.
Arguments:
- starts: float32 [8, 8, 2048, 128], P('slab', 'sub'), may hold values from -6 to 6
- sources: bfloat16 [8, 8, 2048, 128], P('slab', 'sub'), may hold values from -6 to 6
- inverse_conductance: bfloat16 [8, 2048, 2048], P('sub'), as said below
- coarse_decay: float32 [8, 8, 2048], P('slab', 'sub'), as said below
- interface_nodes: int32 [8, 256], P('sub'), may hold values from 0 to 2047, as said below
- retire: int32 [128], replicated, may hold values from 0 to 2, as said below
Outputs:
- window: float32 [8, 8, 2048, 128], P('slab', 'sub')
The draws below stay inside these ranges and needn't reach their ends.
Inputs may be any that keep to these rules, and one draw needn't show every extreme that they name: `interface_nodes`: within each subnetwork the interface nodes are distinct, and 0 and 2047 are in every subnetwork's list. `retire`: some case retires no slab and some retires 2. `coarse_decay`: entries lie in (0, 1]. `inverse_conductance`: each matrix has a positive diagonal.
All inputs are finite; a program needn't handle non-finite values.
Results may differ from the reference program's by a relative error of at most 0.0042.
Values sent between devices are 32-bit elements; how exact they have to be, the bound alone decides.
No kernel may reach another device: no remote copies, remote signals or barrier semaphores. Data moves between devices by JAX's collectives and lax.ppermute only.
A program may use at most 192 MiB of HBM per device.

```python
import jax
import jax.numpy as jnp
from jax import lax

GRID_NODES = 2048
GRID_SUBNETWORKS = 8
CASES = 128
IFACE = 256
STEPS = 8
TIME_SLABS = 8
RMAX = 2


def draw_inverse_conductance(key, part):
    first, second = jax.random.split(key)
    spread = 0.2
    diagonal = jax.random.uniform(first, (GRID_SUBNETWORKS, GRID_NODES), jnp.float32, 0.6, 0.9)
    offdiag = jax.random.normal(second, (GRID_SUBNETWORKS, GRID_NODES, GRID_NODES), jnp.float32) * (spread / GRID_NODES ** 0.5)
    eye = jnp.eye(GRID_NODES, dtype=jnp.float32)
    return (offdiag + diagonal[:, :, None] * eye[None]).astype(jnp.bfloat16)


def draw_coarse_decay(key, part):
    random_keys = jax.random.split(key, 4)
    low = jnp.log(0.1 / TIME_SLABS)
    high = jnp.log(3.0)
    decay_rates = jnp.exp(jax.random.uniform(random_keys[0], (GRID_SUBNETWORKS, GRID_NODES), jnp.float32, low, high))
    random_perturbation = jax.random.uniform(random_keys[1], (TIME_SLABS, GRID_SUBNETWORKS, GRID_NODES), jnp.float32, 0.6, 1.6)
    surge_instant = jax.random.randint(random_keys[2], (2, GRID_SUBNETWORKS, GRID_NODES), 0, TIME_SLABS)
    scale_factor = jax.random.uniform(random_keys[3], (GRID_SUBNETWORKS, GRID_NODES), jnp.float32, 0.5, 0.8)
    slab_indices = jnp.arange(TIME_SLABS)[:, None, None]
    struck_mask = (slab_indices == surge_instant[0][None]) | (slab_indices == surge_instant[1][None])
    surge_pulse = jnp.where(struck_mask, scale_factor[None], 1.0)
    return jnp.exp(-decay_rates[None] * random_perturbation) * surge_pulse


def draw_interface_nodes(key, part):

    def single(sub_key):
        first, second = jax.random.split(sub_key)
        inner = jax.random.permutation(first, GRID_NODES - 2)[:IFACE - 2] + 1
        whole = jnp.concatenate([jnp.array([0, GRID_NODES - 1], dtype=jnp.int32), inner.astype(jnp.int32)])
        order = jax.random.permutation(second, IFACE)
        return whole[order].astype(jnp.int32)
    return jax.vmap(single)(jax.random.split(jax.random.fold_in(key, 11), GRID_SUBNETWORKS))


def draw_retire(key, part):
    first, second = jax.random.split(jax.random.fold_in(key, 23))
    values = jax.random.randint(first, (CASES,), 0, RMAX + 1)
    order = jax.random.permutation(second, CASES)
    values = values.at[order[0]].set(0).at[order[1]].set(RMAX)
    return values.astype(jnp.int32)


def level_of(rng, dims, cuts, smallest, top_value):
    def one(axis_at, shards_of):
        draws = jax.random.uniform(jax.random.fold_in(jax.random.fold_in(rng, 6), axis_at), (shards_of,), jnp.float32, smallest / len(cuts), top_value / len(cuts))
        return jnp.repeat(jnp.exp(draws), dims[axis_at] // shards_of).reshape((-1,) + (1,) * (len(dims) - axis_at - 1))

    level = one(*cuts[0])
    for cut in cuts[1:]:
        level = level * one(*cut)
    return level


def noise(stream_key, shape, width, bound, cuts=(), kind=jnp.bfloat16):
    values = width * jax.random.normal(stream_key, shape, jnp.float32)
    if cuts:
        values = values * level_of(stream_key, shape, cuts, -0.22, 0.18)
    return jnp.clip(values, -bound, bound).astype(kind)


def setup_inputs(seed: int = 0) -> dict:
    key_of = jax.random.split(jax.random.key(seed), 7)
    return {
        "starts": noise(key_of[0], (TIME_SLABS, GRID_SUBNETWORKS, GRID_NODES, CASES), 1.0, 6.0, ((0, 8), (1, 4)), jnp.float32),
        "sources": noise(key_of[1], (TIME_SLABS, GRID_SUBNETWORKS, GRID_NODES, CASES), 1.0, 6.0, ((0, 8), (1, 4))),
        "inverse_conductance": draw_inverse_conductance(jax.random.fold_in(key_of[6], 71), 0),
        "coarse_decay": draw_coarse_decay(jax.random.fold_in(key_of[6], 71), 0),
        "interface_nodes": draw_interface_nodes(jax.random.fold_in(key_of[6], 71), 0),
        "retire": draw_retire(jax.random.fold_in(key_of[6], 71), 0),
    }


def fine_slab(start, source, inverse_conductance, interface_nodes):
    state = start
    source_f = source.astype(jnp.float32)
    for step in range(STEPS):
        stepped = (state + source_f).astype(jnp.bfloat16)
        products = jnp.stack([jnp.dot(inverse_conductance[s], stepped[s], preferred_element_type=jnp.float32) for s in range(GRID_SUBNETWORKS)])
        rows = jax.vmap(lambda block, where_at: block[where_at])(products, interface_nodes)
        mean_iface = jnp.sum(rows, axis=0) / GRID_SUBNETWORKS
        state = jax.vmap(lambda block, where_at: block.at[where_at].set(mean_iface))(products, interface_nodes)
    return state


def reference(starts, sources, inverse_conductance, coarse_decay, interface_nodes, retire):
    fine = lax.map(lambda pair: fine_slab(pair[0], pair[1], inverse_conductance, interface_nodes), (starts, sources))
    correction = fine - coarse_decay[..., None] * starts

    def advance(state, inputs):
        decay_n, corr_n = inputs
        return decay_n[..., None] * state + corr_n, state

    last, states = lax.scan(advance, starts[0], (coarse_decay, correction))
    every = jnp.concatenate([states, last[None]], axis=0)
    position = jnp.arange(TIME_SLABS, dtype=jnp.int32)[:, None] + retire[None, :]
    position = jnp.minimum(position, TIME_SLABS).astype(jnp.int32)
    index = jnp.broadcast_to(position[:, None, None, :], (TIME_SLABS, GRID_SUBNETWORKS, GRID_NODES, CASES))
    return jnp.take_along_axis(every, index, axis=0)
```

```python
import jax
import jax.numpy as jnp
from jax import lax
from jax.experimental import pallas as pl
from jax.experimental.pallas import tpu as pltpu
from jax.sharding import PartitionSpec as P

STEPS = 8
CHUNKS = 4
F32, BF16 = jnp.float32, jnp.bfloat16
VMEM = pl.BlockSpec(memory_space=pltpu.VMEM)
SMEM = pl.BlockSpec(memory_space=pltpu.SMEM)


def shape_of(shape, dtype=F32):
    return jax.ShapeDtypeStruct(shape, dtype)


def dot(a, b):
    return jnp.dot(a, b, preferred_element_type=F32)


def call(kernel, outs, ins, flops=0, **kw):
    params = pltpu.CompilerParams(vmem_limit_bytes=kw.pop("limit", 16 << 20))
    size = sum(o.size * o.dtype.itemsize for o in outs)
    cost = pl.CostEstimate(flops=flops, bytes_accessed=size, transcendentals=0)
    return pl.pallas_call(
        kernel, out_shape=outs, in_specs=ins, out_specs=[VMEM] * len(outs),
        compiler_params=params, cost_estimate=cost, **kw)


def first_kernel(where, a, start, source, z, total, w):
    subs, rows = where.shape
    for s in range(subs):
        w[s] = (start[s] + source[s].astype(F32)).astype(BF16)
        z[s] = dot(a[s], w[s])

    def one(j, carry):
        row = z[0, pl.ds(where[0, j], 1)]
        for s in range(1, subs):
            row = row + z[s, pl.ds(where[s, j], 1)]
        total[pl.ds(j, 1)] = row
        return carry

    lax.fori_loop(0, rows, one, 0, unroll=8)


def pick_kernel(where, a, rows_of_a):
    for s in range(a.shape[0]):
        node = lax.broadcasted_iota(jnp.int32, rows_of_a.shape[1:], 1)
        hot = jnp.where(where[s] == node, 1.0, 0.0).astype(BF16)
        rows_of_a[s] = dot(hot, a[s]).astype(BF16)


def product_kernel(a, w, after, z):
    for s in range(a.shape[0]):
        z[s] = dot(a[s], w[s])


def put_rows(where, mean, z):
    def one(j, carry):
        row = mean[pl.ds(j, 1)]
        for s in range(where.shape[0]):
            z[s, pl.ds(where[s, j], 1)] = row
        return carry

    lax.fori_loop(0, where.shape[1], one, 0, unroll=8)


def next_kernel(count, where, mine, theirs, z, source, rows_of_a, state, w, total, mean):
    mean[...] = (mine[...] + theirs[...]) / count
    put_rows(where, mean, state)
    part = None
    for s in range(z.shape[0]):
        w[s] = (state[s] + source[s].astype(F32)).astype(BF16)
        term = dot(rows_of_a[s], w[s])
        part = term if part is None else part + term
    total[...] = part


def last_kernel(count, where, mine, theirs, z, less, state, mean):
    mean[...] = (mine[...] + theirs[...]) / count
    put_rows(where, mean, state)
    state[...] = state[...] - less[...]


def body(starts, sources, matrix, coarse_decay, interface_nodes, retire):
    start, source, decay = starts[0], sources[0], coarse_decay[0]
    subs, nodes, cases = start.shape
    iface = interface_nodes.shape[1]
    sub_count = lax.axis_size("sub")
    whole = float(subs * sub_count)
    state_t, total_t = shape_of(start.shape), shape_of((iface, cases))
    w_t = shape_of(start.shape, BF16)
    step_flops = 2 * subs * nodes * nodes * cases
    hops = [1 << b for b in range(sub_count.bit_length() - 1)]

    def exchange(total):
        for hop in hops[:-1]:
            total = total + lax.ppermute(total, "sub", [(i, i ^ hop) for i in range(sub_count)])
        theirs = lax.ppermute(total, "sub", [(i, i ^ hops[-1]) for i in range(sub_count)])
        return total, theirs

    position, slabs = lax.axis_index("slab"), lax.axis_size("slab")
    leading = position == 0
    spread = jnp.broadcast_to(decay[..., None], start.shape)
    less = jnp.where(leading, 0.0, spread * start)

    z, total = call(
        first_kernel, [state_t, total_t], [SMEM, VMEM, VMEM, VMEM], step_flops,
        scratch_shapes=[pltpu.VMEM(start.shape, BF16)],
    )(interface_nodes, matrix, start, source)
    (rows_of_a,) = call(
        pick_kernel, [shape_of((subs, iface, nodes), BF16)], [VMEM, VMEM], step_flops,
    )(interface_nodes[:, :, None], matrix)
    mine, theirs = exchange(total)
    for step in range(1, STEPS):
        state, w, total = call(
            lambda *refs: next_kernel(whole, *refs), [state_t, w_t, total_t],
            [SMEM] + [VMEM] * 5, step_flops // 8,
            scratch_shapes=[pltpu.VMEM((iface, cases), F32)],
            input_output_aliases={3: 0},
        )(interface_nodes, mine, theirs, z, source, rows_of_a)
        mine, theirs = exchange(total)
        (z,) = call(product_kernel, [state_t], [VMEM] * 3, step_flops)(matrix, w, mine)
    (correction,) = call(
        lambda *refs: last_kernel(whole, *refs), [state_t], [SMEM] + [VMEM] * 4,
        scratch_shapes=[pltpu.VMEM((iface, cases), F32)],
        input_output_aliases={3: 0},
    )(interface_nodes, mine, theirs, z, less)

    return slab_phase(correction, decay, start, retire)[None]


def slab_phase(correction, decay, start, retire):
    position, slabs = lax.axis_index("slab"), lax.axis_size("slab")
    shape = correction.shape
    cases = shape[-1]
    side, level, levels = position % 2, position // 2, slabs // 2
    swap = [(n, n ^ 1) for n in range(slabs)]
    up = [(n, n + 2) for n in range(slabs - 2)]
    down = [(n + 2, n) for n in range(slabs - 2)]
    half = correction.size // cases // 2
    chunk = half // CHUNKS

    def send(value, pairs):
        return lax.ppermute(value, "slab", pairs)

    def halves(value):
        value = value.reshape((2, half) + value.shape[2:])
        return (
            lax.dynamic_index_in_dim(value, side, 0, False),
            lax.dynamic_index_in_dim(value, 1 - side, 0, False),
        )

    def pair(kept, got):
        return jnp.where(side == 0, kept, got), jnp.where(side == 0, got, kept)

    kept, given = halves(decay)
    first, second = pair(kept, send(given, swap))
    third = send(first, down)
    first = jnp.where(level == 0, 0.0, first)
    first, second, third = (jnp.broadcast_to(d[:, None], (half, cases)) for d in (first, second, third))
    cut = lambda value, k: lax.slice_in_dim(value, k * chunk, (k + 1) * chunk, axis=0)

    kept, given = halves(correction)
    parts = []
    for k in range(CHUNKS):
        c_first, c_second = pair(cut(kept, k), send(cut(given, k), swap))
        c_third = send(c_first, down)
        parts.append((c_first, c_second, c_third))
    both = [cut(first, k) * cut(second, k) for k in range(CHUNKS)]
    offset = [cut(second, k) * parts[k][0] + parts[k][1] for k in range(CHUNKS)]

    def choose(values, t):
        value = values[min(t, CHUNKS - 1)]
        for k in range(min(t, CHUNKS - 1)):
            value = jnp.where(t - level == k, values[k], value)
        return value

    ready = [jnp.zeros((chunk, cases), F32) for _ in range(CHUNKS)]
    for t in range(CHUNKS + levels - 2):
        out = choose(both, t) * choose(ready, t) + choose(offset, t)
        got = send(out, up)
        for k in range(CHUNKS):
            if t + 1 - (levels - 1) <= k <= t:
                ready[k] = jnp.where(level == t + 1 - k, got, ready[k])

    outs = []
    for k in range(CHUNKS):
        c_first, c_second, c_third = parts[k]
        v0 = ready[k]
        v1 = cut(first, k) * v0 + c_first
        v2 = cut(second, k) * v1 + c_second
        v3 = jnp.where(level == levels - 1, v2, cut(third, k) * v2 + c_third)
        w_first = jnp.where(retire == 0, v0, jnp.where(retire == 1, v1, v2))
        w_second = jnp.where(retire == 0, v1, jnp.where(retire == 1, v2, v3))
        stay, leave = pair(w_first, w_second)
        got = send(leave, swap)
        outs.append((stay, got))
    stay = jnp.concatenate([o[0] for o in outs], axis=0)
    got = jnp.concatenate([o[1] for o in outs], axis=0)
    result = jnp.stack(pair(stay, got)).reshape(shape)
    own = jnp.logical_and(position == 0, retire == 0)
    return jnp.where(own[None, None, :], start, result)


def solution(mesh):
    return jax.shard_map(
        body,
        mesh=mesh,
        in_specs=(
            P("slab", "sub", None, None),
            P("slab", "sub", None, None),
            P("sub", None, None),
            P("slab", "sub", None),
            P("sub", None),
            P(),
        ),
        out_specs=P("slab", "sub", None, None),
        check_vma=False,
    )
```

```python
import functools

import jax
import jax.numpy as jnp
from jax import lax
from jax.experimental import pallas as pl
from jax.experimental.pallas import tpu as pltpu
from jax.sharding import PartitionSpec as P

STEPS = 8
CHUNKS = 4
LANES = 128
F32, BF16 = jnp.float32, jnp.bfloat16
VMEM = pl.BlockSpec(memory_space=pltpu.VMEM)
SMEM = pl.BlockSpec(memory_space=pltpu.SMEM)


def shape_of(shape, dtype=F32):
    return jax.ShapeDtypeStruct(shape, dtype)


def dot(a, b):
    return jnp.dot(a, b, preferred_element_type=F32)


def call(kernel, outs, scalars, arrays, flops=0, limit=8 << 20, **kw):
    size = sum(o.size * o.dtype.itemsize for o in outs)
    return pl.pallas_call(
        kernel,
        out_shape=outs,
        in_specs=[SMEM] * len(scalars) + [VMEM] * len(arrays),
        out_specs=[VMEM] * len(outs),
        compiler_params=pltpu.CompilerParams(vmem_limit_bytes=limit),
        cost_estimate=pl.CostEstimate(flops=flops, bytes_accessed=size, transcendentals=0),
        **kw,
    )(*scalars, *arrays)


def first_kernel(pos, where, a, start, source, z, total, w):
    subs, rows = where.shape
    w[...] = (start[...] + source[...].astype(F32)).astype(BF16)

    @pl.loop(0, subs)
    def _(s):
        z[s] = dot(a[s], w[s])

    def one(j, carry):
        row = z[0, pl.ds(where[0, j], 1)]
        for s in range(1, subs):
            row = row + z[s, pl.ds(where[s, j], 1)]
        total[pl.ds(j, 1)] = row
        return carry

    lax.fori_loop(0, rows, one, 0, unroll=8)


def pick_kernel(where, a, rows_of_a):
    node = lax.broadcasted_iota(jnp.int32, rows_of_a.shape[1:], 1)

    @pl.loop(0, a.shape[0])
    def _(s):
        hot = jnp.where(where[s] == node, 1.0, 0.0).astype(BF16)
        rows_of_a[s] = dot(hot, a[s]).astype(BF16)


def product_kernel(a, w, after, z):
    @pl.loop(0, a.shape[0])
    def _(s):
        z[s] = dot(a[s], w[s])


def next_kernel(count, where, mine, theirs, z, source, rows_of_a, state, w, total, mean):
    mean[...] = (mine[...] + theirs[...]) / count

    def one(j, carry):
        row = mean[pl.ds(j, 1)]
        for s in range(where.shape[0]):
            state[s, pl.ds(where[s, j], 1)] = row
        return carry

    lax.fori_loop(0, where.shape[1], one, 0, unroll=8)
    part = None
    for s in range(z.shape[0]):
        w[s] = (state[s] + source[s].astype(F32)).astype(BF16)
        term = dot(rows_of_a[s], w[s])
        part = term if part is None else part + term
    total[...] = part


def last_kernel(count, other, pos, where, mine, theirs, z, less, *rest):
    outs, (state, mean) = rest[:-2], rest[-2:]
    side = pos[0] & 1
    half = 1 - side if other else side
    subs, nodes = z.shape[1:3]
    mean[...] = (mine[...] + theirs[...]) / count
    for h in range(subs):
        state[pl.ds(h * nodes, nodes)] = z[half, h]

    def one(j, carry):
        row = mean[pl.ds(j, 1)]
        for h in range(subs):
            state[pl.ds(h * nodes + where[half * subs + h, j], 1)] = row
        return carry

    lax.fori_loop(0, where.shape[1], one, 0, unroll=8)
    rows = outs[0].shape[0]
    for k, out in enumerate(outs):
        part = pl.ds(k * rows, rows)
        out[...] = state[part] - less[half, part]


def decay_kernel(pos, decay, other, first):
    side = pos[0] & 1
    first[...] = jnp.where(side == 0, decay[side], other[side])


def spread(value, out, factor=None):
    columns = value.T
    for i in range(value.shape[0]):
        part = pl.ds(i * LANES, LANES)
        block = jnp.broadcast_to(columns[:, i:i + 1], (LANES, out.shape[-1]))
        out[part] = block if factor is None else block * factor[part]


def spread_kernel(pos, decay, other, third, start, first_b, second_b, both_b, third_b, less):
    side, level = pos[0] & 1, pos[0] >> 1
    own, got = decay[side], other[side]
    first = jnp.where(side == 0, own, got)
    second = jnp.where(side == 0, got, own)
    first = jnp.where(level == 0, 0.0, first)
    spread(first, first_b)
    spread(second, second_b)
    spread(first * second, both_b)
    spread(third[...], third_b)
    for h in range(2):
        spread(jnp.where(pos[0] == 0, 0.0, decay[h]), less.at[h], start.at[h])


def pair_kernel(k, pos, kept, got, second_b, offset, c_first):
    side = pos[0] & 1
    rows = got.shape[0]
    part = pl.ds(k * rows, rows)
    mine, theirs = kept[part], got[...]
    first = jnp.where(side == 0, mine, theirs)
    second = jnp.where(side == 0, theirs, mine)
    c_first[...] = first
    offset[...] = second_b[part] * first + second


def turn_kernel(turn, count, pos, got, both_b, *rest):
    offsets, out = rest[:-1], rest[-1]
    level = pos[0] >> 1
    rows = out.shape[0]
    for k, offset in enumerate(offsets):
        @pl.when(level == turn - k)
        def _():
            if turn == k:
                out[...] = offset[...]
            else:
                out[...] = both_b[pl.ds(k * rows, rows)] * got[...] + offset[...]


def window_kernel(k, levels, pos, kept, got, c_third, first_b, second_b, third_b, retire, *rest):
    arrived, (stay, leave, value) = rest[:-3], rest[-3:]
    side, level = pos[0] & 1, pos[0] >> 1
    rows = got.shape[0]
    part = pl.ds(k * rows, rows)

    @pl.when(level == 0)
    def _():
        value[...] = jnp.zeros_like(value)

    for z, came in enumerate(arrived):
        @pl.when(level == z + 1)
        def _():
            value[...] = came[...]

    mine, theirs = kept[part], got[...]
    c_first = jnp.where(side == 0, mine, theirs)
    c_second = jnp.where(side == 0, theirs, mine)
    v0 = value[...]
    v1 = first_b[part] * v0 + c_first
    v2 = second_b[part] * v1 + c_second
    v3 = jnp.where(level == levels - 1, v2, third_b[part] * v2 + c_third[...])
    gone = retire[...]
    w_first = jnp.where(gone == 0, v0, jnp.where(gone == 1, v1, v2))
    w_second = jnp.where(gone == 0, v1, jnp.where(gone == 1, v2, v3))
    stay[...] = jnp.where(side == 0, w_first, w_second)
    leave[...] = jnp.where(side == 0, w_second, w_first)


def join_kernel(pos, start, retire, *rest):
    out = rest[-1]
    parts = rest[:-1]
    side = pos[0] & 1
    rows = parts[0].shape[0]
    count = len(parts) // 2
    own = jnp.logical_and(pos[0] == 0, retire[...] == 0)
    for half, group in ((side, parts[:count]), (1 - side, parts[count:])):
        for k, value in enumerate(group):
            part = pl.ds(k * rows, rows)
            out[half, part] = jnp.where(own, start[half, part], value[...])


def body(starts, sources, matrix, coarse_decay, interface_nodes, retire):
    start, source = starts[0], sources[0]
    subs, nodes, cases = start.shape
    iface = interface_nodes.shape[1]
    sub_count, slabs = lax.axis_size("sub"), lax.axis_size("slab")
    whole = float(subs * sub_count)
    state_t, total_t = shape_of(start.shape), shape_of((iface, cases))
    w_t = shape_of(start.shape, BF16)
    step_flops = 2 * subs * nodes * nodes * cases
    hops = [1 << b for b in range(sub_count.bit_length() - 1)]
    half = subs * nodes // 2
    chunk = half // CHUNKS
    levels = slabs // 2
    chunk_t, half_t = shape_of((chunk, cases)), shape_of((half, cases))
    swap = [(n, n ^ 1) for n in range(slabs)]
    up = [(n, n + 2) for n in range(slabs - 2)]
    down = [(n + 2, n) for n in range(slabs - 2)]
    pos = lax.axis_index("slab").reshape(1)
    mean_s = pltpu.VMEM((iface, cases), F32)

    def send(value, pairs):
        return lax.ppermute(value, "slab", pairs)

    def exchange(total):
        for hop in hops[:-1]:
            total = total + lax.ppermute(total, "sub", [(i, i ^ hop) for i in range(sub_count)])
        theirs = lax.ppermute(total, "sub", [(i, i ^ hops[-1]) for i in range(sub_count)])
        return total, theirs

    z, total = call(
        first_kernel, [state_t, total_t], [pos, interface_nodes], [matrix, start, source],
        step_flops, scratch_shapes=[pltpu.VMEM(start.shape, BF16)])
    (rows_of_a,) = call(
        pick_kernel, [shape_of((subs, iface, nodes), BF16)], [],
        [interface_nodes[:, :, None], matrix], step_flops)
    decay = coarse_decay.reshape(2, half // LANES, LANES)
    other = send(decay, swap)
    mine, theirs = exchange(total)
    for step in range(1, STEPS):
        state, w, total = call(
            functools.partial(next_kernel, whole), [state_t, w_t, total_t], [interface_nodes],
            [mine, theirs, z, source, rows_of_a], step_flops // 8,
            scratch_shapes=[mean_s], input_output_aliases={3: 0})
        mine, theirs = exchange(total)
        (z,) = call(product_kernel, [state_t], [], [matrix, w, mine], step_flops)

    (first,) = call(decay_kernel, [shape_of(decay.shape[1:])], [pos], [decay, other])
    halves = start.reshape(2, half, cases)
    first_b, second_b, both_b, third_b, less = call(
        spread_kernel, [half_t] * 4 + [shape_of(halves.shape)], [pos],
        [decay, other, send(first, down), halves])

    split = z.reshape(2, subs // 2, nodes, cases)
    last = functools.partial(
        call, scalars=[pos, interface_nodes], arrays=[mine, theirs, split, less],
        scratch_shapes=[pltpu.VMEM((half, cases), F32), mean_s])
    given = last(functools.partial(last_kernel, whole, True), [chunk_t] * CHUNKS)
    (kept,) = last(functools.partial(last_kernel, whole, False), [half_t])

    got, offsets, thirds = [], [], []
    for k in range(CHUNKS):
        got.append(send(given[k], swap))
        offset, c_first = call(
            functools.partial(pair_kernel, k), [chunk_t] * 2, [pos], [kept, got[k], second_b])
        offsets.append(offset)
        thirds.append(send(c_first, down))
    came = []
    for turn in range(CHUNKS + levels - 2):
        if turn == 0:
            out = offsets[0]
        else:
            (out,) = call(
                functools.partial(turn_kernel, turn, CHUNKS), [chunk_t], [pos],
                [came[-1], both_b] + offsets[:turn + 1])
        came.append(send(out, up))
    gone = retire.reshape(1, cases)
    stays, finals = [], []
    for k in range(CHUNKS):
        stay, leave = call(
            functools.partial(window_kernel, k, levels), [chunk_t] * 2, [pos],
            [kept, got[k], thirds[k], first_b, second_b, third_b, gone] + came[k:k + levels - 1],
            scratch_shapes=[pltpu.VMEM((chunk, cases), F32)])
        stays.append(stay)
        finals.append(send(leave, swap))
    (window,) = call(
        join_kernel, [shape_of(halves.shape)], [pos], [halves, gone] + stays + finals)
    return window.reshape(starts.shape)


def solution(mesh):
    return jax.shard_map(
        body,
        mesh=mesh,
        in_specs=(
            P("slab", "sub", None, None),
            P("slab", "sub", None, None),
            P("sub", None, None),
            P("slab", "sub", None),
            P("sub", None),
            P(),
        ),
        out_specs=P("slab", "sub", None, None),
        check_vma=False,
    )
```
